256 devices in a mesh: seq: 16 (over z, core), ctx: 16 (over y, x).
Axes of the slice: x: 4, y: 4, z: 8, core: 2. Of those that a mesh axis runs over, the one named last changes fastest.
Arguments:
- features: bfloat16 [16, 8192, 2560], P('seq', 'ctx'), may hold values from -6 to 6
- step_sizes: float32 [16, 40, 8192], P('seq', None, 'ctx'), may hold values from 0 to 1, as said below
- rate_logs: float32 [40], replicated, may hold values from -8 to 3
- input_map: bfloat16 [16, 8192, 128], P('seq', 'ctx'), may hold values from -0.5 to 0.5
- output_map: bfloat16 [16, 8192, 128], P('seq', 'ctx'), may hold values from -6 to 6
- skip_gain: float32 [40], replicated, may hold values from 0.5 to 1.5
- state_first: bfloat16 [16, 40, 64, 128], P('seq'), may hold values from -0.5 to 0.5
- upstream: bfloat16 [16, 8192, 2560], P('seq', 'ctx'), may hold values from -45 to 45
- state_last: bfloat16 [16, 40, 64, 128], P('seq'), may hold values from -768 to 768
Outputs:
- grad_features: bfloat16 [16, 8192, 2560], P('seq', 'ctx')
- grad_steps: float32 [16, 40, 8192], P('seq', None, 'ctx')
- grad_input_map: float32 [16, 8192, 128], P('seq', 'ctx')
- grad_output_map: float32 [16, 8192, 128], P('seq', 'ctx')
- grad_rate_logs: float32 [40], replicated
- grad_skip_gain: float32 [40], replicated
The draws below stay inside these ranges and needn't reach their ends.
Inputs may be any that keep to these rules, and one draw needn't show every extreme that they name: `step_sizes`: Positive.
All inputs are finite; a program needn't handle non-finite values.
Results may differ from the reference program's by a relative error of at most 0.0055.
Values sent between devices are 32-bit elements; how exact they have to be, the bound alone decides.
No kernel may reach another device: no remote copies, remote signals or barrier semaphores. Data moves between devices by JAX's collectives and lax.ppermute only.
A program may use at most 192 MiB of HBM per device.

```python
import math
from functools import partial
import jax
import jax.numpy as jnp
from jax import lax

H = 40
P_SIZE = 64
N = 128
Q = 256
TOK_DEV = 512
SEQS = 16
TOKENS = 8192


def draw_step_sizes(key, part):
    base_key, factor_key = jax.random.split(key)
    full_shape = (SEQS, H, TOKENS)
    base_steps = jnp.exp(jax.random.uniform(base_key, full_shape, jnp.float32, math.log(0.25), math.log(4.0)))
    factor = jnp.exp(jax.random.uniform(factor_key, (SEQS, H, TOKENS // TOK_DEV), jnp.float32, -math.log(2.0), math.log(2.0)))
    factor = jnp.repeat(factor, TOK_DEV, axis=2)
    return base_steps * factor / math.sqrt(TOKENS)


def draw_rate_logs(key, part):
    order_key, slow_key, quick_key, middle_key = jax.random.split(key, 4)
    shuffled = jax.random.permutation(order_key, H)
    quick_count = max(1, H // 10)
    middle_count = 3 * H // 10
    slow_rate = jnp.exp(jax.random.uniform(slow_key, (H,), jnp.float32, math.log(0.2), math.log(1.4))) / math.sqrt(TOKENS)
    quick_rate = jnp.exp(jax.random.uniform(quick_key, (H,), jnp.float32, math.log(1.0 / 75.0), math.log(1.0 / 45.0))) * math.sqrt(TOKENS)
    middle_rate = jnp.exp(jax.random.uniform(middle_key, (H,), jnp.float32, math.log(0.6), math.log(1.2))) * math.sqrt(TOKENS) / TOK_DEV
    is_quick = shuffled < quick_count
    is_middle = jnp.logical_and(shuffled >= quick_count, shuffled < quick_count + middle_count)
    rates = jnp.where(is_quick, quick_rate, jnp.where(is_middle, middle_rate, slow_rate))
    return jnp.log(rates)


def draw_upstream(key, part):
    noise_key = jax.random.fold_in(key, 0)
    full_shape = (SEQS, TOKENS, H * P_SIZE)
    gaussian = jax.random.truncated_normal(noise_key, -6.0, 6.0, full_shape, jnp.float32)
    sequence_ramp = 1.0 + 2.0 * jnp.arange(SEQS, dtype=jnp.float32) / SEQS
    token_ramp = 1.0 + 2.0 * jnp.arange(TOKENS, dtype=jnp.float32) / TOKENS
    divisor = 3.0
    values = gaussian * sequence_ramp[:, None, None] * token_ramp[None, :, None] / divisor
    return values.astype(jnp.bfloat16)


def level_of(stream_key, extent, pieces, smallest, high):
    def one(dim, parts):
        draws = jax.random.uniform(jax.random.fold_in(jax.random.fold_in(stream_key, 6), dim), (parts,), jnp.float32, smallest / len(pieces), high / len(pieces))
        return jnp.repeat(jnp.exp(draws), extent[dim] // parts).reshape((-1,) + (1,) * (len(extent) - dim - 1))

    level = one(*pieces[0])
    for cut in pieces[1:]:
        level = level * one(*cut)
    return level


def normal_values(stream_key, extent, deviation, most, pieces=(), kind=jnp.bfloat16):
    values = deviation * jax.random.normal(stream_key, extent, jnp.float32)
    if pieces:
        values = values * level_of(stream_key, extent, pieces, -0.22, 0.18)
    return jnp.clip(values, -most, most).astype(kind)


def setup_inputs(seed: int = 0) -> dict:
    seeds = jax.random.split(jax.random.key(seed), 10)
    return {
        "features": normal_values(seeds[0], (SEQS, TOKENS, H * P_SIZE), 1.0, 6.0, ((0, 16), (1, 16))),
        "step_sizes": draw_step_sizes(jax.random.fold_in(seeds[9], 71), 0),
        "rate_logs": draw_rate_logs(jax.random.fold_in(seeds[9], 71), 0),
        "input_map": normal_values(seeds[3], (SEQS, TOKENS, N), N ** -0.5, 0.5, ((0, 16), (1, 16))),
        "output_map": normal_values(seeds[4], (SEQS, TOKENS, N), 1.0, 6.0, ((0, 16), (1, 16))),
        "skip_gain": jnp.clip(jax.random.uniform(seeds[5], (H,), jnp.float32, 0.5, 1.5), 0.5, 1.5),
        "state_first": normal_values(seeds[6], (SEQS, H, P_SIZE, N), N ** -0.5, 0.5, ((0, 16),)),
        "upstream": draw_upstream(jax.random.fold_in(seeds[9], 71), 0),
        "state_last": normal_values(seeds[8], (SEQS, H, P_SIZE, N), (TOK_DEV // 4), 768.0, ((0, 16),)),
    }


def split_blocks(features, step_sizes, input_map, output_map, upstream, head_count):
    length = features.shape[0]
    blocks = length // Q
    head_size = features.shape[1] // head_count
    return (features.reshape(blocks, Q, head_count, head_size),
            jnp.transpose(step_sizes.reshape(head_count, blocks, Q), (1, 0, 2)),
            input_map.reshape(blocks, Q, -1),
            output_map.reshape(blocks, Q, -1),
            upstream.reshape(blocks, Q, head_count, head_size))


def block_local(block_data, decay_rates):
    inputs, steps, map_in, map_out, upstream = block_data
    log_sums = jnp.cumsum(steps * decay_rates[:, None], axis=1)
    end_logs = log_sums[:, Q - 1]
    scaled = jnp.exp(end_logs[:, None] - log_sums) * steps
    decayed_in = (inputs.astype(jnp.float32) * jnp.transpose(scaled)[:, :, None]).astype(jnp.bfloat16)
    decayed_up = (upstream.astype(jnp.float32) * jnp.exp(jnp.transpose(log_sums))[:, :, None]).astype(jnp.bfloat16)
    fresh_block = jnp.einsum("shp,sn->hpn", decayed_in, map_in, preferred_element_type=jnp.float32)
    readout = jnp.einsum("thp,tn->hpn", decayed_up, map_out, preferred_element_type=jnp.float32)
    scores = jnp.dot(map_out, map_in.T, preferred_element_type=jnp.float32)
    inner_dots = jnp.einsum("thp,shp->hts", upstream, inputs, preferred_element_type=jnp.float32)
    causal = jnp.arange(Q)[:, None] >= jnp.arange(Q)[None, :]
    spread = jnp.minimum(log_sums[:, :, None] - log_sums[:, None, :], 0.0)
    kernel = jnp.where(causal[None], jnp.exp(spread), 0.0) * scores[None]
    mixing = (kernel * steps[:, None, :]).astype(jnp.bfloat16)
    grad_inputs = jnp.einsum("hts,thp->shp", mixing, upstream, preferred_element_type=jnp.float32)
    weighted = kernel * inner_dots
    pulled = weighted * steps[:, None, :]
    score_grads = jnp.sum(pulled, axis=0).astype(jnp.bfloat16)
    grad_in = jnp.dot(score_grads.T, map_out, preferred_element_type=jnp.float32)
    grad_out = jnp.dot(score_grads, map_in, preferred_element_type=jnp.float32)
    log_grads = jnp.sum(pulled, axis=2) - jnp.sum(pulled, axis=1)
    step_grads = jnp.sum(weighted, axis=1)
    skip_part = jnp.sum(jnp.diagonal(inner_dots, axis1=1, axis2=2), axis=1)
    return (log_sums, scaled, decayed_in, decayed_up, fresh_block, readout,
            grad_inputs, grad_in, grad_out, log_grads, step_grads, skip_part)


def enter_block(running, element):
    end_log, fresh_block = element
    return jnp.exp(end_log)[:, None, None] * running + fresh_block, running


def finish_block(block_data, decay_rates, skip_gain):
    (inputs, steps, map_in, map_out, upstream, log_sums, scaled, decayed_in, decayed_up,
     entering, leaving, grad_inputs, grad_in, grad_out, log_grads, step_grads) = block_data
    end_logs = log_sums[:, Q - 1]
    entering_half = entering.astype(jnp.bfloat16)
    leaving_half = leaving.astype(jnp.bfloat16)
    carried_out = jnp.einsum("tn,hpn->thp", map_out, entering_half, preferred_element_type=jnp.float32)
    carried_in = jnp.einsum("sn,hpn->shp", map_in, leaving_half, preferred_element_type=jnp.float32)
    upstream_wide = upstream.astype(jnp.float32)
    readout_dots = jnp.transpose(jnp.sum(upstream_wide * carried_out, axis=2))
    input_dots = jnp.transpose(jnp.sum(inputs.astype(jnp.float32) * carried_in, axis=2))
    scaled_rows = jnp.transpose(scaled)[:, :, None]
    features_grad = grad_inputs + scaled_rows * carried_in + skip_gain[None, :, None] * upstream_wide
    in_grad = grad_in + jnp.einsum("shp,hpn->sn", decayed_in, leaving_half, preferred_element_type=jnp.float32)
    out_grad = grad_out + jnp.einsum("thp,hpn->tn", decayed_up, entering_half, preferred_element_type=jnp.float32)
    fresh_terms = scaled * input_dots
    end_extra = jnp.sum(fresh_terms, axis=1) + jnp.exp(end_logs) * jnp.sum(leaving * entering, axis=(1, 2))
    last_token = (jnp.arange(Q) == Q - 1).astype(jnp.float32)
    total_logs = log_grads + jnp.exp(log_sums) * readout_dots - fresh_terms + end_extra[:, None] * last_token[None, :]
    through = jnp.flip(jnp.cumsum(jnp.flip(total_logs, 1), axis=1), 1)
    steps_grad = decay_rates[:, None] * through + step_grads + jnp.exp(end_logs[:, None] - log_sums) * input_dots
    rate_part = jnp.sum(steps * through, axis=1)
    return features_grad, steps_grad, in_grad, out_grad, rate_part


def region_finish(stacked, local_parts, decay_rates, skip_gain, state_in, cot_out):
    end_logs = local_parts[0][:, :, Q - 1]
    _, entering = lax.scan(enter_block, state_in, (end_logs, local_parts[4]))
    _, leaving = lax.scan(enter_block, cot_out, (end_logs, local_parts[5]), reverse=True)
    block_data = stacked + local_parts[:4] + (entering, leaving) + local_parts[6:11]
    return lax.map(partial(finish_block, decay_rates=decay_rates, skip_gain=skip_gain), block_data)


def assemble(finished, local_parts, length, head_count):
    features_grad = finished[0].reshape(length, -1)
    steps_grad = jnp.transpose(finished[1], (1, 0, 2)).reshape(head_count, length)
    in_grad = finished[2].reshape(length, -1)
    out_grad = finished[3].reshape(length, -1)
    rate_sum = jnp.sum(finished[4], axis=0)
    skip_sum = jnp.sum(local_parts[11], axis=0)
    return features_grad, steps_grad, in_grad, out_grad, rate_sum, skip_sum


def sequence_grads(seq_data, decay_rates, skip_gain):
    features, step_sizes, input_map, output_map, state_first, upstream, state_last = seq_data
    head_count = decay_rates.shape[0]
    length = features.shape[0]
    stacked = split_blocks(features, step_sizes, input_map, output_map, upstream, head_count)
    local_parts = lax.map(partial(block_local, decay_rates=decay_rates), stacked)
    finished = region_finish(stacked, local_parts, decay_rates, skip_gain,
                             state_first.astype(jnp.float32), state_last.astype(jnp.float32))
    return assemble(finished, local_parts, length, head_count)


def reference(features, step_sizes, rate_logs, input_map, output_map, skip_gain, state_first, upstream, state_last):
    decay_rates = -jnp.exp(rate_logs)
    results = lax.map(partial(sequence_grads, decay_rates=decay_rates, skip_gain=skip_gain),
                      (features, step_sizes, input_map, output_map, state_first, upstream, state_last))
    return (results[0].astype(jnp.bfloat16), results[1], results[2], results[3],
            decay_rates * jnp.sum(results[4], axis=0), jnp.sum(results[5], axis=0))
```

```python
from functools import partial

import jax
import jax.numpy as jnp
from jax import lax
from jax.experimental import pallas as pl
from jax.experimental.pallas import tpu as pltpu
from jax.sharding import PartitionSpec as P

Q = 256
HG = 8
PS = 64
NS = 128
GC = HG * PS
LOG2E = 1.4426950408889634
PARTS = ((0, 3), (3, 2))
HI = lax.Precision.HIGHEST
F32 = jnp.float32
BF16 = jnp.bfloat16
VLIM = 56 * 1024 * 1024


def nt(a, b, **kw):
    return lax.dot_general(a, b, (((1,), (1,)), ((), ())), preferred_element_type=F32, **kw)


def tn(a, b):
    return lax.dot_general(a, b, (((0,), (0,)), ((), ())), preferred_element_type=F32)


def nn(a, b, **kw):
    return lax.dot_general(a, b, (((1,), (0,)), ((), ())), preferred_element_type=F32, **kw)


def iota(shape, dim):
    return lax.broadcasted_iota(jnp.int32, shape, dim)


def tri():
    return (iota((Q, Q), 0) <= iota((Q, Q), 1)).astype(F32)


def split3(v):
    hi = v.astype(BF16).astype(F32)
    rest = v - hi
    mid = rest.astype(BF16).astype(F32)
    return [hi, mid, rest - mid]


def head_sel(rows):
    return (iota((rows, GC), 0) % HG == iota((rows, GC), 1) // PS).astype(BF16)


def expand(v):
    stacked = jnp.concatenate(split3(v), axis=0)
    return tn(stacked.astype(BF16), head_sel(3 * HG))


def part_kernel(idx, x_ref, g_ref, st_ref, rl_ref, mi_ref, mo_ref, p0, p1, p2, p3, f0_ref, r1_ref, en_ref, fs, rs):
    col = lax.bitwise_and(idx[0], 3)
    rate = -jnp.exp(rl_ref[...])
    upper = tri()
    fresh, readout, ends = [], [], []
    for c in range(2):
        rows = slice(c * Q, (c + 1) * Q)
        dt = st_ref[:, rows]
        sums = nn(dt * rate, upper, precision=HI)
        end = sums[:, Q - 1 :]
        scaled = expand(jnp.exp(end - sums) * dt)
        grown = expand(jnp.exp(sums))
        din = (x_ref[rows, :].astype(F32) * scaled).astype(BF16)
        dup = (g_ref[rows, :].astype(F32) * grown).astype(BF16)
        fresh.append(tn(mi_ref[rows, :], din))
        readout.append(tn(mo_ref[rows, :], dup))
        ends.append(grown[Q - 1 :, :])
    fs[...] = ends[1] * fresh[0] + fresh[1]
    rs[...] = readout[0] + ends[0] * readout[1]
    f0_ref[...] = fresh[0]
    r1_ref[...] = readout[1]
    en_ref[0:8, :] = jnp.broadcast_to(ends[0], (8, GC))
    en_ref[8:16, :] = jnp.broadcast_to(ends[1], (8, GC))
    decay = jnp.broadcast_to(ends[0] * ends[1], (8, GC))
    for k, out in enumerate((p0, p1, p2, p3)):
        start = pl.multiple_of(lax.bitwise_xor(col, k) * 32, 32)
        out[0:32, :] = fs[pl.ds(start, 32), :]
        out[32:64, :] = rs[pl.ds(start, 32), :]
        out[64:72, :] = decay


def const_spec(shape):
    return pl.BlockSpec(shape, lambda g, i: (0, 0))


def col_spec(rows, width, g0=0):
    return pl.BlockSpec((rows, width), lambda g, i: (0, g + g0))


def row_spec(width, g0=0):
    return pl.BlockSpec((HG, width), lambda g, i: (g + g0, 0))


def run_part(idx, x, g, st, rl, mi, mo, g0, ng):
    tok, width = x.shape[0], ng * GC
    shapes = [(72, width)] * 4 + [(NS, width)] * 2 + [(16, width)]
    return pl.pallas_call(
        part_kernel,
        out_shape=[jax.ShapeDtypeStruct(s, F32) for s in shapes],
        grid_spec=pltpu.PrefetchScalarGridSpec(
            num_scalar_prefetch=1,
            grid=(ng,),
            in_specs=[
                col_spec(tok, GC, g0),
                col_spec(tok, GC, g0),
                row_spec(tok, g0),
                row_spec(1, g0),
                const_spec((tok, NS)),
                const_spec((tok, NS)),
            ],
            out_specs=[col_spec(s[0], GC) for s in shapes],
            scratch_shapes=[pltpu.VMEM((NS, GC), F32), pltpu.VMEM((NS, GC), F32)],
        ),
        compiler_params=pltpu.CompilerParams(vmem_limit_bytes=VLIM),
        cost_estimate=pl.CostEstimate(
            flops=8 * tok * NS * width, bytes_accessed=8 * tok * width, transcendentals=0
        ),
        name="states",
    )(idx, x, g, st, rl, mi, mo)


def quad_kernel(x_ref, g_ref, st_ref, rl_ref, mi_ref, mo_ref, gx_ref, ll_ref, sl_ref, gi_ref, go_ref, sk_ref, sc, sg):
    grp = pl.program_id(1)

    @pl.when(grp == 0)
    def _():
        causal = iota((Q, Q), 0) <= iota((Q, Q), 1)
        sc[...] = jnp.where(causal, nt(mi_ref[...], mo_ref[...]), 0.0)
        sg[...] = jnp.zeros((Q, Q), F32)

    dt = st_ref[...]
    rate = -jnp.exp(rl_ref[...])
    sums = nn(dt * rate, tri(), precision=HI) * LOG2E
    sums_col, dt_col = sums.T, dt.T
    lane = iota((Q, 128), 1)
    low = lane < PS
    cols = jnp.zeros((Q, 128), F32)
    a, b = slice(0, 128), slice(128, 256)
    for pr in range(HG // 2):
        cs = slice(128 * pr, 128 * (pr + 1))
        xp, gp = x_ref[:, cs], g_ref[:, cs]
        skip = xp.astype(F32) * gp.astype(F32)
        sk_ref[:, cs] = jnp.sum(skip.reshape(Q // 8, 8, 128), axis=0)
        outs = []
        for hh in range(2):
            j = 2 * pr + hh
            xm = jnp.where(low if hh == 0 else jnp.logical_not(low), xp, jnp.zeros_like(xp))
            top = nt(xm[a], gp)
            bot = nt(xm[b], gp[b])
            lr, lc, dc = sums[j : j + 1, :], sums_col[:, j : j + 1], dt_col[:, j : j + 1]
            k00 = jnp.exp2(jnp.minimum(lr[:, a] - lc[a], 0.0)) * sc[a, a]
            k01 = jnp.exp2(jnp.minimum(lr[:, b] - lc[a], 0.0)) * sc[a, b]
            k11 = jnp.exp2(jnp.minimum(lr[:, b] - lc[b], 0.0)) * sc[b, b]
            m00, m01, m11 = k00 * dc[a], k01 * dc[a], k11 * dc[b]
            i00, i01 = top[:, a], top[:, b]
            p00, p01, p11 = m00 * i00, m01 * i01, m11 * bot
            sg[a, a] += p00
            sg[a, b] += p01
            sg[b, b] += p11
            ll_ref[j : j + 1, a] = jnp.sum(p00, axis=0, keepdims=True)
            ll_ref[j : j + 1, b] = jnp.sum(p01 + p11, axis=0, keepdims=True)
            wt = jnp.sum(k00 * i00 + k01 * i01, axis=1, keepdims=True)
            wb = jnp.sum(k11 * bot, axis=1, keepdims=True)
            cols = jnp.where(lane == j, jnp.concatenate([wt, wb], axis=0), cols)
            mt = jnp.concatenate([m00.astype(BF16), m01.astype(BF16)], axis=1)
            outs.append(jnp.concatenate([nn(mt, gp), nn(m11.astype(BF16), gp[b])], axis=0))
        gx_ref[:, cs] = jnp.where(low, outs[0], outs[1])
    step_part = cols.T[0:HG, :]
    sl_ref[...] = step_part
    ll_ref[...] = ll_ref[...] - dt * step_part

    @pl.when(grp == pl.num_programs(1) - 1)
    def _():
        grads = sg[...].astype(BF16)
        gi_ref[...] = nn(grads, mo_ref[...])
        go_ref[...] = tn(grads, mi_ref[...])


def run_quad(x, g, st, rl, mi, mo):
    tok, width = x.shape
    blocks, groups = tok // Q, width // GC
    heads = st.shape[0]
    cg = lambda r, w: pl.BlockSpec((r, w), lambda c, g: (c, g))
    gc = lambda w: pl.BlockSpec((HG, w), lambda c, g: (g, c))
    cc = pl.BlockSpec((Q, NS), lambda c, g: (c, 0))
    return pl.pallas_call(
        quad_kernel,
        out_shape=[
            jax.ShapeDtypeStruct((tok, width), F32),
            jax.ShapeDtypeStruct((heads, tok), F32),
            jax.ShapeDtypeStruct((heads, tok), F32),
            jax.ShapeDtypeStruct((tok, NS), F32),
            jax.ShapeDtypeStruct((tok, NS), F32),
            jax.ShapeDtypeStruct((8 * blocks, width), F32),
        ],
        grid=(blocks, groups),
        in_specs=[
            cg(Q, GC),
            cg(Q, GC),
            gc(Q),
            pl.BlockSpec((HG, 1), lambda c, g: (g, 0)),
            cc,
            cc,
        ],
        out_specs=[cg(Q, GC), gc(Q), gc(Q), cc, cc, cg(8, GC)],
        scratch_shapes=[pltpu.VMEM((Q, Q), F32), pltpu.VMEM((Q, Q), F32)],
        compiler_params=pltpu.CompilerParams(vmem_limit_bytes=VLIM),
        cost_estimate=pl.CostEstimate(
            flops=30 * tok * Q * width, bytes_accessed=8 * tok * width, transcendentals=tok * Q * heads
        ),
        name="quad",
    )(x, g, st, rl, mi, mo)


def product(terms):
    out = None
    for t in terms:
        out = t if out is None else out * t
    return out


def pick(cond, v):
    return jnp.where(cond, v, 1.0)


def weighted(cond, w, v):
    return jnp.where(cond, w, 0.0) * v


def row_kernel(idx, r0, r1, r2, r3, o1, o2, o3):
    me = idx[0]
    col, row = lax.bitwise_and(me, 3), lax.shift_right_logical(me, 2)
    refs = (r0, r1, r2, r3)
    pos = [lax.bitwise_xor(col, k) for k in range(4)]
    dec = [r[64:65, :] for r in refs]
    fwd = bwd = 0.0
    for k in range(4):
        others = [k2 for k2 in range(4) if k2 != k]
        fwd = fwd + product([pick(pos[k2] > pos[k], dec[k2]) for k2 in others]) * refs[k][0:32, :]
        bwd = bwd + product([pick(pos[k2] < pos[k], dec[k2]) for k2 in others]) * refs[k][32:64, :]
    total = jnp.broadcast_to(product(dec), (8, GC))
    for m, out in zip((1, 2, 3), (o1, o2, o3)):
        out[0:32, :] = jnp.where(lax.bitwise_xor(row, m) > row, fwd, bwd)
        out[32:40, :] = total


def spread_kernel(idx, r0, r1, r2, r3, y1, y2, y3, sf, sl, o0, o1, o2, o3):
    me = idx[0]
    col, row = lax.bitwise_and(me, 3), lax.shift_right_logical(me, 2)
    ys = (y1, y2, y3)
    ypos = [lax.bitwise_xor(row, m) for m in (1, 2, 3)]
    ydec = [r[32:33, :] for r in ys]
    enter = product([pick(ypos[m] < row, ydec[m]) for m in range(3)]) * sf[...].astype(F32)
    leave = product([pick(ypos[m] > row, ydec[m]) for m in range(3)]) * sl[...].astype(F32)
    for m in range(3):
        others = [m2 for m2 in range(3) if m2 != m]
        below, above = ypos[m] < row, ypos[m] > row
        wf = product([pick((ypos[m2] > ypos[m]) & (ypos[m2] < row), ydec[m2]) for m2 in others])
        wb = product([pick((ypos[m2] < ypos[m]) & (ypos[m2] > row), ydec[m2]) for m2 in others])
        enter = enter + jnp.where(below, wf * ys[m][0:32, :], 0.0)
        leave = leave + jnp.where(above, wb * ys[m][0:32, :], 0.0)
    refs, outs = (r0, r1, r2, r3), (o0, o1, o2, o3)
    pos = [lax.bitwise_xor(col, k) for k in range(4)]
    dec = [r[64:65, :] for r in refs]
    for k in range(4):
        others = [k2 for k2 in range(4) if k2 != k]
        pre = product([pick(pos[k2] < pos[k], dec[k2]) for k2 in others]) * enter
        suf = product([pick(pos[k2] > pos[k], dec[k2]) for k2 in others]) * leave
        for k2 in others:
            mid = [k3 for k3 in others if k3 != k2]
            wf = product([pick((pos[k3] > pos[k2]) & (pos[k3] < pos[k]), dec[k3]) for k3 in mid])
            wb = product([pick((pos[k3] < pos[k2]) & (pos[k3] > pos[k]), dec[k3]) for k3 in mid])
            pre = pre + jnp.where(pos[k2] < pos[k], wf * refs[k2][0:32, :], 0.0)
            suf = suf + jnp.where(pos[k2] > pos[k], wb * refs[k2][32:64, :], 0.0)
        outs[k][0:32, :] = pre
        outs[k][32:64, :] = suf


def run_cols(body, name, idx, ins, out_rows, width):
    return pl.pallas_call(
        body,
        out_shape=[jax.ShapeDtypeStruct((r, width), F32) for r in out_rows],
        grid_spec=pltpu.PrefetchScalarGridSpec(
            num_scalar_prefetch=1,
            grid=(width // GC,),
            in_specs=[col_spec(a.shape[0], GC) for a in ins],
            out_specs=[col_spec(r, GC) for r in out_rows],
        ),
        compiler_params=pltpu.CompilerParams(vmem_limit_bytes=VLIM),
        cost_estimate=pl.CostEstimate(flops=100 * 32 * width, bytes_accessed=2000 * width, transcendentals=0),
        name=name,
    )(idx, *ins)


def group_sums(v):
    sel = head_sel(16)[0:8]
    hi = v.astype(BF16)
    lo = (v - hi.astype(F32)).astype(BF16)
    return nt(sel, hi) + nt(sel, lo)


def finish_body(
    idx, x_ref, g_ref, st_ref, rl_ref, mi_ref, mo_ref, s0, s1, s2, s3, f0_ref, r1_ref, en_ref, gx_ref, ll_ref, sl_ref,
    gi_ref, go_ref, sk_ref, of_ref, os_ref, oi_ref, oo_ref, orr_ref, es, ls,
):
    grp = pl.program_id(0)
    col = lax.bitwise_and(idx[0], 3)
    for k, ref in enumerate((s0, s1, s2, s3)):
        start = pl.multiple_of(lax.bitwise_xor(col, k) * 32, 32)
        es[pl.ds(start, 32), :] = ref[0:32, :]
        ls[pl.ds(start, 32), :] = ref[32:64, :]

    @pl.when(grp == 0)
    def _():
        oi_ref[...] = gi_ref[...]
        oo_ref[...] = go_ref[...]

    rate = -jnp.exp(rl_ref[...])
    upper = tri()
    first, last = es[...], ls[...]
    entering = [first, en_ref[0:1, :] * first + f0_ref[...]]
    leaving = [en_ref[8:9, :] * last + r1_ref[...], last]
    is_end = iota((HG, Q), 1) == Q - 1
    rate_sum = jnp.zeros((HG, 1), F32)
    for c in range(2):
        rows = slice(c * Q, (c + 1) * Q)
        dt = st_ref[:, rows]
        sums = nn(dt * rate, upper, precision=HI)
        end = sums[:, Q - 1 :]
        ratio = jnp.exp(end - sums)
        grow = jnp.exp(sums)
        scaled = ratio * dt
        scaled_wide, grow_wide = expand(scaled), expand(grow)
        ent, lea = entering[c].astype(BF16), leaving[c].astype(BF16)
        carried_out = nn(mo_ref[rows, :], ent)
        carried_in = nn(mi_ref[rows, :], lea)
        xw, gw = x_ref[rows, :].astype(F32), g_ref[rows, :].astype(F32)
        read_dots = group_sums(gw * carried_out)
        input_dots = group_sums(xw * carried_in)
        of_ref[rows, :] = (gx_ref[rows, :] + scaled_wide * carried_in + sk_ref[...] * gw).astype(BF16)
        din = (xw * scaled_wide).astype(BF16)
        dup = (gw * grow_wide).astype(BF16)
        oi_ref[rows, :] += nt(din, lea)
        oo_ref[rows, :] += nt(dup, ent)
        pair = jnp.sum(leaving[c] * entering[c], axis=0, keepdims=True)
        both = nt(head_sel(8).astype(F32), jnp.broadcast_to(pair, (8, GC)), precision=HI)[:, 0:1]
        fresh = scaled * input_dots
        extra = jnp.sum(fresh, axis=1, keepdims=True) + jnp.exp(end) * both
        logs = ll_ref[:, rows] + grow * read_dots - fresh + jnp.where(is_end, extra, 0.0)
        through = nt(logs, upper, precision=HI)
        os_ref[:, rows] = rate * through + sl_ref[:, rows] + ratio * input_dots
        rate_sum = rate_sum + jnp.sum(dt * through, axis=1, keepdims=True)
    orr_ref[...] = jnp.broadcast_to(rate_sum, (HG, 128))


def finish_kernel(n_alias, *refs):
    n_in = 21
    finish_body(*refs[: n_in - 1], *refs[n_in - 1 + n_alias :])


def run_finish(idx, x, g, st, rl, mi, mo, back, f0, r1, en, gx, ll, sl, gi, go, skip, prev, g0, ng):
    tok, width = x.shape
    heads = st.shape[0]
    alias = [] if prev is None else list(prev)
    rate_in = [] if prev is None else []
    ins = [x, g, st, rl, mi, mo, *back, f0, r1, en, gx, ll, sl, gi, go, skip]
    specs = [
        col_spec(tok, GC, g0),
        col_spec(tok, GC, g0),
        row_spec(tok, g0),
        row_spec(1, g0),
        const_spec((tok, NS)),
        const_spec((tok, NS)),
        *[col_spec(64, GC)] * 4,
        col_spec(NS, GC),
        col_spec(NS, GC),
        col_spec(16, GC),
        col_spec(tok, GC, g0),
        row_spec(tok, g0),
        row_spec(tok, g0),
        const_spec((tok, NS)),
        const_spec((tok, NS)),
        col_spec(1, GC, g0),
    ]
    base = 1 + len(ins)
    return pl.pallas_call(
        partial(finish_kernel, len(alias)),
        out_shape=[
            jax.ShapeDtypeStruct((tok, width), BF16),
            jax.ShapeDtypeStruct((heads, tok), F32),
            jax.ShapeDtypeStruct((tok, NS), F32),
            jax.ShapeDtypeStruct((tok, NS), F32),
            jax.ShapeDtypeStruct((ng * HG, 128), F32),
        ],
        grid_spec=pltpu.PrefetchScalarGridSpec(
            num_scalar_prefetch=1,
            grid=(ng,),
            in_specs=specs + [pl.BlockSpec(memory_space=pl.ANY)] * len(alias),
            out_specs=[
                col_spec(tok, GC, g0),
                row_spec(tok, g0),
                const_spec((tok, NS)),
                const_spec((tok, NS)),
                row_spec(128),
            ],
            scratch_shapes=[pltpu.VMEM((NS, GC), F32), pltpu.VMEM((NS, GC), F32)],
        ),
        input_output_aliases={base + i: i for i in range(len(alias))},
        compiler_params=pltpu.CompilerParams(vmem_limit_bytes=VLIM),
        cost_estimate=pl.CostEstimate(
            flops=8 * tok * NS * ng * GC, bytes_accessed=10 * tok * ng * GC, transcendentals=0
        ),
        name="finish",
    )(idx, *ins, *alias)


def along_x(value, k):
    return lax.ppermute(value, "ctx", [(i, i ^ k) for i in range(16)])


def along_y(value, m):
    return lax.ppermute(value, "ctx", [(i, i ^ (4 * m)) for i in range(16)])


def sent_to_all(value, axis):
    copies = jnp.broadcast_to(value, (lax.axis_size(axis), *value.shape))
    return lax.all_to_all(copies, axis, split_axis=0, concat_axis=0, tiled=True)


def taken_together(value, axis):
    return jnp.sum(sent_to_all(value, axis), axis=0)


def state_slice(state, col, g0, ng):
    flat = state.reshape(-1, NS)[g0 * GC : (g0 + ng) * GC]
    return lax.dynamic_slice(flat.T, (col * 32, 0), (32, ng * GC))


def local(x, st, rate_logs, mi, mo, skip_gain, first, g, final):
    x, st, mi, mo, g, first, final = x[0], st[0], mi[0], mo[0], g[0], first[0], final[0]
    me = lax.axis_index("ctx").astype(jnp.int32)
    idx = me.reshape(1)
    col = me & 3
    rl = rate_logs.reshape(-1, 1)
    skip = jnp.repeat(skip_gain, PS)[None]
    got, kept = [], []
    for g0, ng in PARTS:
        *pay, f0, r1, en = run_part(idx, x, g, st, rl, mi, mo, g0, ng)
        kept.append((f0, r1, en))
        got.append([pay[0]] + [along_x(pay[k], k) for k in (1, 2, 3)])
    gx, ll, sl, gi, go, sk = run_quad(x, g, st, rl, mi, mo)
    rows = []
    for (g0, ng), recv in zip(PARTS, got):
        sends = run_cols(row_kernel, "row", idx, recv, (40, 40, 40), ng * GC)
        rows.append([along_y(v, m) for v, m in zip(sends, (1, 2, 3))])
    backs = []
    for (g0, ng), recv, ys in zip(PARTS, got, rows):
        sf = state_slice(first, col, g0, ng)
        sl_ = state_slice(final, col, g0, ng)
        outs = run_cols(spread_kernel, "spread", idx, [*recv, *ys, sf, sl_], (64,) * 4, ng * GC)
        backs.append([outs[0]] + [along_x(outs[k], k) for k in (1, 2, 3)])
    skip_local = jnp.sum(sk, axis=0).reshape(-1, PS).sum(axis=1)
    prev, rates = None, []
    gin, gout = gi, go
    for (g0, ng), back, keep in zip(PARTS, backs, kept):
        of, os, oi, oo, rr = run_finish(
            idx, x, g, st, rl, mi, mo, back, *keep, gx, ll, sl, gin, gout, skip, prev, g0, ng
        )
        prev, gin, gout = (of, os), oi, oo
        rates.append(rr[:, 0])
    both = jnp.concatenate([*rates, skip_local])
    total = taken_together(taken_together(both, "ctx"), "seq")
    heads = rate_logs.shape[0]
    return (of[None], os[None], oi[None], oo[None], -jnp.exp(rate_logs) * total[:heads], total[heads:])


def solution(mesh):
    return jax.shard_map(
        local,
        mesh=mesh,
        in_specs=(
            P("seq", "ctx", None),
            P("seq", None, "ctx"),
            P(),
            P("seq", "ctx", None),
            P("seq", "ctx", None),
            P(),
            P("seq", None, None, None),
            P("seq", "ctx", None),
            P("seq", None, None, None),
        ),
        out_specs=(
            P("seq", "ctx", None),
            P("seq", None, "ctx"),
            P("seq", "ctx", None),
            P("seq", "ctx", None),
            P(),
            P(),
        ),
        check_vma=False,
    )
```
